32 devices in a mesh: sec: 8 (over y, x, core), op: 4 (over z).
Axes of the slice: x: 2, y: 2, z: 4, core: 2. Of those that a mesh axis runs over, the one named last changes fastest.
Arguments:
- environment: float32 [8, 56, 256, 256], P('sec', 'op'), may hold values from -6 to 6
- mps: float32 [8, 4, 256, 256], P('sec'), may hold values from -0.375 to 0.375
- mpo: float32 [56, 4, 56], P('op'), may hold values from -0.75 to 0.75
- mpo_pattern: int32 [56, 4], P('op'), may hold values 0 or 1
- state_shift: int32 [4], replicated, may hold values from 0 to 7, as said below
- sector_dims: int32 [8], replicated, may hold values from 1 to 256, 1024 in all
Outputs:
- new_environment: float32 [8, 56, 4, 256], P('sec', 'op')
The draws below stay inside these ranges and needn't reach their ends.
Inputs may be any that keep to these rules, and one draw needn't show every extreme that they name: `state_shift`: the four shifts are 0, 1, 4 and 7, assigned to the physical states in an order drawn from the seed. `sector_dims`: the live states sum to 1024.
All inputs are finite; a program needn't handle non-finite values. No bound on the sum of `mpo_pattern` on one device may be relied on, other than what follows from the above.
Results may differ from the reference program's by a relative error of at most 0.000088.
Values sent between devices are 32-bit elements; how exact they have to be, the bound alone decides.
No kernel may reach another device: no remote copies, remote signals or barrier semaphores. Data moves between devices by JAX's collectives and lax.ppermute only.
A program may use at most 64 MiB of HBM per device.

```python
import math
import jax
import jax.numpy as jnp
import numpy as np
from jax import lax

SECT = 256
PHYS = 4
ROWS = 4
SECTORS = 8
CHANNELS = 56


def draw_state_shift(key, part):
    values = jnp.array([0, 1, SECTORS // 2, SECTORS - 1], dtype=jnp.int32)
    order = jax.random.permutation(jax.random.fold_in(key, 17), PHYS)
    return values[order].astype(jnp.int32)


def touch_ends(values, key, low, largest):
    longest = values.shape.index(max(values.shape))
    spots = []
    for shift in (0, 1):
        where = [jax.random.randint(jax.random.fold_in(key, axis), (), 0, length) for axis, length in enumerate(values.shape)]
        where[longest] = (where[longest] + shift) % values.shape[longest]
        spots.append(tuple(where))
    return values.at[spots[0]].set(low).at[spots[1]].set(largest)


def spiked(entries, stream_key, source, target, parts, factor):
    owner, partner = [(jnp.arange(entries.shape[position]) // (entries.shape[position] // parts)).reshape([-1 if axis == position else 1 for axis in range(entries.ndim)]) for position in (source, target)]
    chosen = jax.random.permutation(stream_key, parts)[partner]
    strong = (owner == chosen) | (owner == (partner + parts // 2) % parts)
    return jnp.where(strong, factor * entries, entries)


def block_scale(key, extent, pieces, low, top_value):
    def one(position, blocks):
        steps = jax.random.uniform(jax.random.fold_in(jax.random.fold_in(key, 6), position), (blocks,), jnp.float32, low / len(pieces), top_value / len(pieces))
        return jnp.repeat(jnp.exp(steps), extent[position] // blocks).reshape((-1,) + (1,) * (len(extent) - position - 1))

    factor_of = one(*pieces[0])
    for cut in pieces[1:]:
        factor_of = factor_of * one(*cut)
    return factor_of


def split_up(amount, total, bound, slope):
    loads = [(1 << 20) // math.isqrt(grade ** slope) + 1 for grade in range(2, amount + 1)]
    surplus, holding = total - bound - (amount - 1), [1] * (amount - 1)
    while surplus > 0:
        movable = [i for i in range(amount - 1) if holding[i] < bound]
        whole, remaining = sum([loads[i] for i in movable]), surplus
        for i in movable:
            addition = min(bound - holding[i], max(1, remaining * loads[i] // whole), surplus)
            holding[i] = holding[i] + addition
            surplus = surplus - addition
    return np.array([bound] + holding)


def uneven_parts(key, amount, total, reach, skew):
    if amount == 2:
        one = jax.random.randint(key, (), max(1, total - reach), min(reach, total - 1) + 1)
        return jnp.stack([one, total - one])
    tallies = jnp.asarray(split_up(amount, total, reach, skew), jnp.int32)
    couples = (amount - 1) // 2
    giver, taker = tallies[1:1 + 2 * couples:2], tallies[2:2 + 2 * couples:2]
    margin = jnp.minimum(giver - 1, reach - taker)
    moved = jax.random.randint(jax.random.fold_in(key, 1), (couples,), 0, 1 << 20) % (margin + 1)
    tallies = tallies.at[1:1 + 2 * couples:2].set(giver - moved).at[2:2 + 2 * couples:2].set(taker + moved)
    return tallies[jax.random.permutation(jax.random.fold_in(key, 2), amount)]


def noise(rng, shape, deviation, limit, pieces=(), held_as=jnp.bfloat16):
    gain = block_scale(rng, shape, pieces, -0.22, 0.18) if pieces else 1.0
    drawn = jax.random.normal(rng, shape, jnp.float32) * deviation * gain
    return jnp.minimum(jnp.maximum(drawn, -limit), limit).astype(held_as)


def bell_draw_with(key, dims, scale, limit, pieces, heavy, kind=jnp.bfloat16):
    values = scale * jax.random.normal(key, dims, jnp.float32)
    if pieces:
        values = values * block_scale(key, dims, pieces, -0.22, 0.18)
    return jnp.clip(spiked(values, jax.random.fold_in(key, 3), *heavy), -limit, limit).astype(kind)


def setup_inputs(seed: int = 0) -> dict:
    key_of = jax.random.split(jax.random.key(seed), 7)
    environment = noise(key_of[0], (SECTORS, CHANNELS, SECT, SECT), 1.0, 6.0, ((0, 8), (1, 4)), jnp.float32)
    mps = noise(key_of[1], (SECTORS, PHYS, SECT, SECT), SECT ** -0.5, 0.375, ((0, 8),), jnp.float32)
    mpo = bell_draw_with(key_of[2], (CHANNELS, PHYS, CHANNELS), (CHANNELS * PHYS // 2) ** -0.5, 0.75, ((0, 4),), (0, 2, 4, 2.0), jnp.float32)
    mpo_pattern = touch_ends((jax.random.randint(key_of[3], (CHANNELS, PHYS), 0, 2) < 1).astype(jnp.int32), jax.random.fold_in(key_of[3], 1), 0, 1)
    state_shift = draw_state_shift(jax.random.fold_in(key_of[6], 71), 0)
    sector_dims = uneven_parts(key_of[5], SECTORS, SECTORS * SECT // 2, SECT, 2).astype(jnp.int32)
    return dict(environment=environment, mps=mps, mpo=mpo, mpo_pattern=mpo_pattern, state_shift=state_shift, sector_dims=sector_dims)


def reference(environment, mps, mpo, mpo_pattern, state_shift, sector_dims):
    highest = lax.Precision.HIGHEST
    sectors = environment.shape[0]
    positions = jnp.arange(SECT, dtype=jnp.int32)
    indices = jnp.arange(sectors, dtype=jnp.int32)
    target = ((indices[:, None] + state_shift[None, :]) % sectors).astype(jnp.int32)
    live_in = (positions[None, :] < sector_dims[:, None]).astype(jnp.float32)
    live_out = (positions[None, None, :] < sector_dims[target][:, :, None]).astype(jnp.float32)
    masked = mps * live_in[:, None, :, None] * live_out[:, :, None, :]

    def transform(operands):
        tensor, block_env = operands
        left = tensor[:, :, :ROWS]
        half = jnp.einsum("sar,wab->swrb", left, block_env, precision=highest)
        return jnp.einsum("swrb,sbc->swrc", half, tensor, precision=highest)

    blocks = lax.map(transform, (masked, environment))
    coef = mpo * mpo_pattern[:, :, None].astype(jnp.float32)
    source = ((indices[:, None] - state_shift[None, :]) % sectors).astype(jnp.int32)

    def assemble(anchor):
        picked = jnp.stack([blocks[anchor[state], state] for state in range(PHYS)])
        return jnp.einsum("swrc,wsv->vrc", picked, coef, precision=highest)

    return lax.map(assemble, source)
```

```python
import jax
import jax.numpy as jnp
from jax import lax
from jax.sharding import PartitionSpec as P

ROWS = 4
EXCHANGE = "permute"


def shifted(value, axis, steps):
    count = lax.axis_size(axis)
    pairs = [(source, (source + steps) % count) for source in range(count)]
    return lax.ppermute(value, axis, pairs)


def local(environment, mps, mpo, mpo_pattern, state_shift, sector_dims):
    highest = lax.Precision.HIGHEST
    sectors = lax.axis_size("sec")
    here = lax.axis_index("sec")
    parts = lax.axis_size("op")
    me = lax.axis_index("op")
    width = mps.shape[-1]
    states = mps.shape[1]
    positions = jnp.arange(width, dtype=jnp.int32)
    labels = jnp.arange(sectors, dtype=jnp.int32)
    target = (here + state_shift) % sectors
    dims_out = jnp.sum(
        jnp.where(target[:, None] == labels[None, :], sector_dims[None, :], 0), axis=1
    )
    dims_in = jnp.sum(jnp.where(labels == here, sector_dims, 0))
    live_in = (positions < dims_in).astype(jnp.float32)
    live_out = (positions[None, :] < dims_out[:, None]).astype(jnp.float32)
    masked = mps[0] * live_in[None, :, None] * live_out[:, None, :]
    left = masked[:, :, :ROWS]
    half = jnp.einsum("sar,wab->swrb", left, environment[0], precision=highest)
    blocks = jnp.einsum("swrb,sbc->swrc", half, masked, precision=highest)
    steps = (0, 1, sectors // 2, sectors - 1)
    ids = jnp.arange(states, dtype=jnp.int32)
    picks = [jnp.sum(jnp.where(state_shift % sectors == step, ids, 0)) for step in steps]
    routed = []
    for step, pick in zip(steps, picks):
        block = lax.dynamic_index_in_dim(blocks, pick, 0, keepdims=False)
        routed.append(block if step == 0 else shifted(block, "sec", step))
    coef = mpo * mpo_pattern[:, :, None].astype(jnp.float32)
    chosen = jnp.stack([lax.dynamic_index_in_dim(coef, pick, 1, keepdims=False) for pick in picks])
    partial = jnp.einsum("kwrc,kwv->vrc", jnp.stack(routed), chosen, precision=highest)
    chunk = partial.shape[0] // parts
    pieces = partial.reshape((parts, chunk) + partial.shape[1:])
    if EXCHANGE == "permute":
        total = lax.dynamic_index_in_dim(pieces, me, 0, keepdims=False)
        for step in range(1, parts):
            send = lax.dynamic_index_in_dim(pieces, (me + step) % parts, 0, keepdims=False)
            total = total + shifted(send, "op", step)
    else:
        total = jnp.sum(lax.all_to_all(pieces, "op", 0, 0, tiled=True), axis=0)
    return total[None]


def solution(mesh):
    in_specs = (
        P("sec", "op", None, None),
        P("sec", None, None, None),
        P("op", None, None),
        P("op", None),
        P(),
        P(),
    )
    out_specs = P("sec", "op", None, None)
    return jax.shard_map(local, mesh=mesh, in_specs=in_specs, out_specs=out_specs, check_vma=False)
```

```python
import functools

import jax
import jax.numpy as jnp
from jax import lax
from jax.experimental import pallas as pl
from jax.experimental.pallas import tpu as pltpu
from jax.sharding import PartitionSpec as P

ROWS = 4
PRECISION = lax.Precision.HIGHEST


def shifted(value, axis, steps):
    count = lax.axis_size(axis)
    pairs = [(source, (source + steps) % count) for source in range(count)]
    return lax.ppermute(value, axis, pairs)


def sector_steps(sectors):
    return (0, 1, sectors // 2, sectors - 1)


def transform_kernel(here_ref, dims_ref, shift_ref, env_ref, mps_ref, coef_ref,
                     blocks_ref, chosen_ref, masked_sc, left_sc, half_sc):
    sectors = dims_ref.shape[0]
    states = mps_ref.shape[1]
    channels = env_ref.shape[1]
    width = mps_ref.shape[-1]
    here = here_ref[0]
    dims_in = dims_ref[here]
    rows = lax.broadcasted_iota(jnp.int32, (width, width), 0)
    cols = lax.broadcasted_iota(jnp.int32, (width, width), 1)
    for k, step in enumerate(sector_steps(sectors)):
        pick = 0
        for s in range(states):
            pick = pick + jnp.where(lax.rem(shift_ref[s], sectors) == step, s, 0)
        dims_out = dims_ref[lax.rem(here + step, sectors)]
        live = (rows < dims_in) & (cols < dims_out)
        masked = jnp.where(live, mps_ref[0, pick], 0.0)
        masked_sc[k] = masked
        left_sc[k * ROWS:(k + 1) * ROWS, :] = jnp.transpose(masked[:, :128])[:ROWS]
        chosen_ref[k] = coef_ref[pick]
    left = left_sc[...]
    for j in range(channels):
        half = jnp.dot(left, env_ref[0, j], precision=PRECISION,
                       preferred_element_type=jnp.float32)
        for k in range(states):
            half_sc[k, j * ROWS:(j + 1) * ROWS, :] = half[k * ROWS:(k + 1) * ROWS]
    for k in range(states):
        full = jnp.dot(half_sc[k], masked_sc[k], precision=PRECISION,
                       preferred_element_type=jnp.float32)
        for j in range(channels):
            blocks_ref[k, j] = full[j * ROWS:(j + 1) * ROWS]


def transform(here, sector_dims, state_shift, environment, mps, coef_t):
    channels, width = environment.shape[1], environment.shape[-1]
    states = mps.shape[1]
    smem = pl.BlockSpec(memory_space=pltpu.SMEM)
    vmem = pl.BlockSpec(memory_space=pltpu.VMEM)
    flops = 2 * states * ROWS * width * width * channels * 2
    return pl.pallas_call(
        transform_kernel,
        out_shape=(
            jax.ShapeDtypeStruct((states, channels, ROWS, width), jnp.float32),
            jax.ShapeDtypeStruct(coef_t.shape, jnp.float32),
        ),
        in_specs=[smem, smem, smem, vmem, vmem, vmem],
        out_specs=(vmem, vmem),
        scratch_shapes=[
            pltpu.VMEM((states, width, width), jnp.float32),
            pltpu.VMEM((states * ROWS, width), jnp.float32),
            pltpu.VMEM((states, channels * ROWS, width), jnp.float32),
        ],
        compiler_params=pltpu.CompilerParams(vmem_limit_bytes=48 * 1024 * 1024),
        cost_estimate=pl.CostEstimate(
            flops=6 * flops, transcendentals=0,
            bytes_accessed=4 * (environment.size + mps.size + 2 * states * channels * ROWS * width)),
    )(here, sector_dims, state_shift, environment, mps, coef_t)


def local(environment, mps, mpo, mpo_pattern, state_shift, sector_dims):
    highest = lax.Precision.HIGHEST
    sectors = lax.axis_size("sec")
    parts = lax.axis_size("op")
    me = lax.axis_index("op")
    here = lax.axis_index("sec").astype(jnp.int32).reshape(1)
    coef_t = jnp.transpose(mpo * mpo_pattern[:, :, None].astype(jnp.float32), (1, 0, 2))
    blocks, chosen = transform(here, sector_dims, state_shift, environment, mps, coef_t)
    routed = [blocks[0]]
    for k, step in enumerate(sector_steps(sectors)):
        if k:
            routed.append(shifted(blocks[k], "sec", step))
    partial = jnp.einsum("kwrc,kwv->vrc", jnp.stack(routed), chosen, precision=highest)
    chunk = partial.shape[0] // parts
    pieces = partial.reshape((parts, chunk) + partial.shape[1:])
    total = lax.dynamic_index_in_dim(pieces, me, 0, keepdims=False)
    for step in range(1, parts):
        send = lax.dynamic_index_in_dim(pieces, (me + step) % parts, 0, keepdims=False)
        total = total + shifted(send, "op", step)
    return total[None]


def solution(mesh):
    in_specs = (
        P("sec", "op", None, None),
        P("sec", None, None, None),
        P("op", None, None),
        P("op", None),
        P(),
        P(),
    )
    out_specs = P("sec", "op", None, None)
    return jax.shard_map(local, mesh=mesh, in_specs=in_specs, out_specs=out_specs, check_vma=False)
```

```python
import jax
import jax.numpy as jnp
from jax import lax
from jax.experimental import pallas as pl
from jax.experimental.pallas import tpu as pltpu
from jax.sharding import PartitionSpec as P

ROWS = 4
PRECISION = lax.Precision.HIGHEST


def shifted(value, axis, steps):
    count = lax.axis_size(axis)
    pairs = [(source, (source + steps) % count) for source in range(count)]
    return lax.ppermute(value, axis, pairs)


def sector_steps(sectors):
    return (0, 1, sectors // 2, sectors - 1)


def transform_kernel(dims_hbm, shift_hbm, env_hbm, mps_hbm, *refs):
    count = len(refs) - 8
    onehot_ref, dims_sc, shift_sc, mps_sc, env_sc, masked_sc, left_sc, half_sc, sems = refs[count - 1:]
    blocks_refs = refs[:count - 1]
    sectors = dims_sc.shape[0]
    states = mps_sc.shape[0]
    channels = env_sc.shape[0]
    width = mps_sc.shape[-1]
    small = [
        pltpu.make_async_copy(dims_hbm, dims_sc, sems.at[0]),
        pltpu.make_async_copy(shift_hbm, shift_sc, sems.at[1]),
        pltpu.make_async_copy(mps_hbm.at[0], mps_sc, sems.at[2]),
    ]
    for copy in small:
        copy.start()
    loads = []
    for j in range(channels):
        copy = pltpu.make_async_copy(env_hbm.at[0, j], env_sc.at[j], sems.at[3 + j])
        copy.start()
        loads.append(copy)
    for copy in small:
        copy.wait()
    here = lax.axis_index("sec")
    dims_in = dims_sc[here]
    rows = lax.broadcasted_iota(jnp.int32, (width, width), 0)
    cols = lax.broadcasted_iota(jnp.int32, (width, width), 1)
    lanes = lax.broadcasted_iota(jnp.int32, (1, states), 1)
    for k, step in enumerate(sector_steps(sectors)):
        pick = 0
        for s in range(states):
            pick = pick + jnp.where(lax.rem(shift_sc[s], sectors) == step, s, 0)
        dims_out = dims_sc[lax.rem(here + step, sectors)]
        live = (rows < dims_in) & (cols < dims_out)
        masked = jnp.where(live, mps_sc[pick], 0.0)
        masked_sc[k] = masked
        left_sc[k * ROWS:(k + 1) * ROWS, :] = jnp.transpose(masked[:, :128])[:ROWS]
        onehot_ref[k:k + 1, :] = (lanes == pick).astype(jnp.float32)
    left = left_sc[...]
    for j in range(channels):
        loads[j].wait()
        half = jnp.dot(left, env_sc[j], precision=PRECISION,
                       preferred_element_type=jnp.float32)
        for k in range(states):
            half_sc[k, j * ROWS:(j + 1) * ROWS, :] = half[k * ROWS:(k + 1) * ROWS]
    for k in range(states):
        full = jnp.dot(half_sc[k], masked_sc[k], precision=PRECISION,
                       preferred_element_type=jnp.float32)
        for j in range(channels):
            blocks_refs[k][j] = full[j * ROWS:(j + 1) * ROWS]


def transform(sector_dims, state_shift, environment, mps):
    channels, width = environment.shape[1], environment.shape[-1]
    states = mps.shape[1]
    anywhere = pl.BlockSpec(memory_space=pl.ANY)
    vmem = pl.BlockSpec(memory_space=pltpu.VMEM)
    flops = 2 * states * ROWS * width * width * channels * 2
    return pl.pallas_call(
        transform_kernel,
        out_shape=tuple(
            jax.ShapeDtypeStruct((channels, ROWS, width), jnp.float32) for _ in range(states)
        ) + (jax.ShapeDtypeStruct((states, states), jnp.float32),),
        in_specs=[anywhere] * 4,
        out_specs=(vmem,) * (states + 1),
        scratch_shapes=[
            pltpu.SMEM(sector_dims.shape, jnp.int32),
            pltpu.SMEM(state_shift.shape, jnp.int32),
            pltpu.VMEM((states, width, width), jnp.float32),
            pltpu.VMEM((channels, width, width), jnp.float32),
            pltpu.VMEM((states, width, width), jnp.float32),
            pltpu.VMEM((states * ROWS, width), jnp.float32),
            pltpu.VMEM((states, channels * ROWS, width), jnp.float32),
            pltpu.SemaphoreType.DMA((3 + channels,)),
        ],
        cost_estimate=pl.CostEstimate(
            flops=6 * flops, transcendentals=0,
            bytes_accessed=4 * (environment.size + mps.size + states * channels * ROWS * width)),
    )(sector_dims, state_shift, environment, mps)


def local(environment, mps, mpo, mpo_pattern, state_shift, sector_dims):
    highest = lax.Precision.HIGHEST
    sectors = lax.axis_size("sec")
    parts = lax.axis_size("op")
    me = lax.axis_index("op")
    *blocks, onehot = transform(sector_dims, state_shift, environment, mps)
    routed = [blocks[0]]
    for k, step in enumerate(sector_steps(sectors)):
        if k:
            routed.append(shifted(blocks[k], "sec", step))
    coef = mpo * mpo_pattern[:, :, None].astype(jnp.float32)
    chosen = jnp.sum(onehot[:, None, :, None] * coef[None], axis=2)
    partial = jnp.einsum("kwrc,kwv->vrc", jnp.stack(routed), chosen, precision=highest)
    chunk = partial.shape[0] // parts
    pieces = partial.reshape((parts, chunk) + partial.shape[1:])
    total = lax.dynamic_index_in_dim(pieces, me, 0, keepdims=False)
    for step in range(1, parts):
        send = lax.dynamic_index_in_dim(pieces, (me + step) % parts, 0, keepdims=False)
        total = total + shifted(send, "op", step)
    return total[None]


def solution(mesh):
    in_specs = (
        P("sec", "op", None, None),
        P("sec", None, None, None),
        P("op", None, None),
        P("op", None),
        P(),
        P(),
    )
    out_specs = P("sec", "op", None, None)
    return jax.shard_map(local, mesh=mesh, in_specs=in_specs, out_specs=out_specs, check_vma=False)
```

```python
import jax
import jax.numpy as jnp
from jax import lax
from jax.experimental import pallas as pl
from jax.experimental.pallas import tpu as pltpu
from jax.sharding import PartitionSpec as P

ROWS = 4
PRECISION = lax.Precision.HIGH


def shifted(value, axis, steps):
    count = lax.axis_size(axis)
    pairs = [(source, (source + steps) % count) for source in range(count)]
    return lax.ppermute(value, axis, pairs)


def sector_steps(sectors):
    return (0, 1, sectors // 2, sectors - 1)


def transform_kernel(dims_hbm, shift_hbm, env_hbm, mps_hbm, *refs):
    count = len(refs) - 8
    onehot_ref, dims_sc, shift_sc, mps_sc, env_sc, masked_sc, left_sc, half_sc, sems = refs[count - 1:]
    blocks_refs = refs[:count - 1]
    sectors = dims_sc.shape[0]
    states = mps_sc.shape[0]
    channels = env_sc.shape[0]
    width = mps_sc.shape[-1]
    small = [
        pltpu.make_async_copy(dims_hbm, dims_sc, sems.at[0]),
        pltpu.make_async_copy(shift_hbm, shift_sc, sems.at[1]),
        pltpu.make_async_copy(mps_hbm.at[0], mps_sc, sems.at[2]),
    ]
    for copy in small:
        copy.start()
    loads = []
    for j in range(channels):
        copy = pltpu.make_async_copy(env_hbm.at[0, j], env_sc.at[j], sems.at[3 + j])
        copy.start()
        loads.append(copy)
    for copy in small:
        copy.wait()
    here = lax.axis_index("sec")
    dims_in = dims_sc[here]
    rows = lax.broadcasted_iota(jnp.int32, (width, width), 0)
    cols = lax.broadcasted_iota(jnp.int32, (width, width), 1)
    lanes = lax.broadcasted_iota(jnp.int32, (1, states), 1)
    for k, step in enumerate(sector_steps(sectors)):
        pick = 0
        for s in range(states):
            pick = pick + jnp.where(lax.rem(shift_sc[s], sectors) == step, s, 0)
        dims_out = dims_sc[lax.rem(here + step, sectors)]
        live = (rows < dims_in) & (cols < dims_out)
        masked = jnp.where(live, mps_sc[pick], 0.0)
        masked_sc[k] = masked
        left_sc[k * ROWS:(k + 1) * ROWS, :] = jnp.transpose(masked[:, :128])[:ROWS]
        onehot_ref[k:k + 1, :] = (lanes == pick).astype(jnp.float32)
    left = left_sc[...]
    for j in range(channels):
        loads[j].wait()
        half = jnp.dot(left, env_sc[j], precision=PRECISION,
                       preferred_element_type=jnp.float32)
        for k in range(states):
            half_sc[k, j * ROWS:(j + 1) * ROWS, :] = half[k * ROWS:(k + 1) * ROWS]
    for k in range(states):
        full = jnp.dot(half_sc[k], masked_sc[k], precision=PRECISION,
                       preferred_element_type=jnp.float32)
        for j in range(channels):
            blocks_refs[k][j] = full[j * ROWS:(j + 1) * ROWS]


def transform(sector_dims, state_shift, environment, mps):
    channels, width = environment.shape[1], environment.shape[-1]
    states = mps.shape[1]
    anywhere = pl.BlockSpec(memory_space=pl.ANY)
    vmem = pl.BlockSpec(memory_space=pltpu.VMEM)
    flops = 2 * states * ROWS * width * width * channels * 2
    return pl.pallas_call(
        transform_kernel,
        out_shape=tuple(
            jax.ShapeDtypeStruct((channels, ROWS, width), jnp.float32) for _ in range(states)
        ) + (jax.ShapeDtypeStruct((states, states), jnp.float32),),
        in_specs=[anywhere] * 4,
        out_specs=(vmem,) * (states + 1),
        scratch_shapes=[
            pltpu.SMEM(sector_dims.shape, jnp.int32),
            pltpu.SMEM(state_shift.shape, jnp.int32),
            pltpu.VMEM((states, width, width), jnp.float32),
            pltpu.VMEM((channels, width, width), jnp.float32),
            pltpu.VMEM((states, width, width), jnp.float32),
            pltpu.VMEM((states * ROWS, width), jnp.float32),
            pltpu.VMEM((states, channels * ROWS, width), jnp.float32),
            pltpu.SemaphoreType.DMA((3 + channels,)),
        ],
        cost_estimate=pl.CostEstimate(
            flops=6 * flops, transcendentals=0,
            bytes_accessed=4 * (environment.size + mps.size + states * channels * ROWS * width)),
    )(sector_dims, state_shift, environment, mps)


def local(environment, mps, mpo, mpo_pattern, state_shift, sector_dims):
    highest = lax.Precision.HIGHEST
    sectors = lax.axis_size("sec")
    parts = lax.axis_size("op")
    me = lax.axis_index("op")
    *blocks, onehot = transform(sector_dims, state_shift, environment, mps)
    routed = [blocks[0]]
    for k, step in enumerate(sector_steps(sectors)):
        if k:
            routed.append(shifted(blocks[k], "sec", step))
    coef = mpo * mpo_pattern[:, :, None].astype(jnp.float32)
    chosen = jnp.sum(onehot[:, None, :, None] * coef[None], axis=2)
    partial = jnp.einsum("kwrc,kwv->vrc", jnp.stack(routed), chosen, precision=highest)
    chunk = partial.shape[0] // parts
    pieces = partial.reshape((parts, chunk) + partial.shape[1:])
    total = lax.dynamic_index_in_dim(pieces, me, 0, keepdims=False)
    for step in range(1, parts):
        send = lax.dynamic_index_in_dim(pieces, (me + step) % parts, 0, keepdims=False)
        total = total + shifted(send, "op", step)
    return total[None]


def solution(mesh):
    in_specs = (
        P("sec", "op", None, None),
        P("sec", None, None, None),
        P("op", None, None),
        P("op", None),
        P(),
        P(),
    )
    out_specs = P("sec", "op", None, None)
    return jax.shard_map(local, mesh=mesh, in_specs=in_specs, out_specs=out_specs, check_vma=False)
```

```python
import jax
import jax.numpy as jnp
from jax import lax
from jax.experimental import pallas as pl
from jax.experimental.pallas import tpu as pltpu
from jax.sharding import PartitionSpec as P

ROWS = 4
PRECISION = lax.Precision.HIGH


def shifted(value, axis, steps):
    count = lax.axis_size(axis)
    pairs = [(source, (source + steps) % count) for source in range(count)]
    return lax.ppermute(value, axis, pairs)


def sector_steps(sectors):
    return (0, 1, sectors // 2, sectors - 1)


def transform_kernel(dims_hbm, shift_hbm, env_hbm, mps_hbm, *refs):
    count = len(refs) - 8
    onehot_ref, dims_sc, shift_sc, mps_sc, env_sc, masked_sc, left_sc, half_sc, sems = refs[count - 1:]
    blocks_refs = refs[:count - 1]
    sectors = dims_sc.shape[0]
    states = mps_sc.shape[0]
    channels = env_sc.shape[0]
    width = mps_sc.shape[-1]
    small = [
        pltpu.make_async_copy(dims_hbm, dims_sc, sems.at[0]),
        pltpu.make_async_copy(shift_hbm, shift_sc, sems.at[1]),
        pltpu.make_async_copy(mps_hbm.at[0], mps_sc, sems.at[2]),
    ]
    for copy in small:
        copy.start()
    loads = []
    for j in range(channels):
        copy = pltpu.make_async_copy(env_hbm.at[0, j], env_sc.at[j], sems.at[3 + j])
        copy.start()
        loads.append(copy)
    for copy in small:
        copy.wait()
    here = lax.axis_index("sec")
    dims_in = dims_sc[here]
    rows = lax.broadcasted_iota(jnp.int32, (width, width), 0)
    cols = lax.broadcasted_iota(jnp.int32, (width, width), 1)
    lanes = lax.broadcasted_iota(jnp.int32, (1, states), 1)
    for k, step in enumerate(sector_steps(sectors)):
        pick = 0
        for s in range(states):
            pick = pick + jnp.where(lax.rem(shift_sc[s], sectors) == step, s, 0)
        dims_out = dims_sc[lax.rem(here + step, sectors)]
        live = (rows < dims_in) & (cols < dims_out)
        masked = jnp.where(live, mps_sc[pick], 0.0)
        masked_sc[k] = masked
        left_sc[k * ROWS:(k + 1) * ROWS, :] = jnp.transpose(masked[:, :128])[:ROWS]
        onehot_ref[k:k + 1, :] = (lanes == pick).astype(jnp.float32)
    left = left_sc[...]
    for j in range(channels):
        loads[j].wait()
        half = jnp.dot(left, env_sc[j], precision=PRECISION,
                       preferred_element_type=jnp.float32)
        for k in range(states):
            half_sc[k, j * ROWS:(j + 1) * ROWS, :] = half[k * ROWS:(k + 1) * ROWS]
    for k in range(states):
        full = jnp.dot(half_sc[k], masked_sc[k], precision=PRECISION,
                       preferred_element_type=jnp.float32)
        for j in range(channels):
            blocks_refs[k][j] = full[j * ROWS:(j + 1) * ROWS]


def transform(sector_dims, state_shift, environment, mps):
    channels, width = environment.shape[1], environment.shape[-1]
    states = mps.shape[1]
    anywhere = pl.BlockSpec(memory_space=pl.ANY)
    vmem = pl.BlockSpec(memory_space=pltpu.VMEM)
    flops = 2 * states * ROWS * width * width * channels * 2
    return pl.pallas_call(
        transform_kernel,
        out_shape=tuple(
            jax.ShapeDtypeStruct((channels, ROWS, width), jnp.float32) for _ in range(states)
        ) + (jax.ShapeDtypeStruct((states, states), jnp.float32),),
        in_specs=[anywhere] * 4,
        out_specs=(vmem,) * (states + 1),
        scratch_shapes=[
            pltpu.SMEM(sector_dims.shape, jnp.int32),
            pltpu.SMEM(state_shift.shape, jnp.int32),
            pltpu.VMEM((states, width, width), jnp.float32),
            pltpu.VMEM((channels, width, width), jnp.float32),
            pltpu.VMEM((states, width, width), jnp.float32),
            pltpu.VMEM((states * ROWS, width), jnp.float32),
            pltpu.VMEM((states, channels * ROWS, width), jnp.float32),
            pltpu.SemaphoreType.DMA((3 + channels,)),
        ],
        cost_estimate=pl.CostEstimate(
            flops=6 * flops, transcendentals=0,
            bytes_accessed=4 * (environment.size + mps.size + states * channels * ROWS * width)),
    )(sector_dims, state_shift, environment, mps)


def local(environment, mps, mpo, mpo_pattern, state_shift, sector_dims):
    highest = lax.Precision.HIGHEST
    sectors = lax.axis_size("sec")
    parts = lax.axis_size("op")
    me = lax.axis_index("op")
    *blocks, onehot = transform(sector_dims, state_shift, environment, mps)
    routed = [blocks[0]]
    for k, step in enumerate(sector_steps(sectors)):
        if k:
            routed.append(shifted(blocks[k], "sec", step))
    coef = mpo * mpo_pattern[:, :, None].astype(jnp.float32)
    chosen = jnp.sum(onehot[:, None, :, None] * coef[None], axis=2)
    partial = None
    for k, block in enumerate(routed):
        term = jnp.einsum("wrc,wv->vrc", block, chosen[k], precision=highest)
        partial = term if partial is None else partial + term
    chunk = partial.shape[0] // parts
    pieces = partial.reshape((parts, chunk) + partial.shape[1:])
    total = lax.dynamic_index_in_dim(pieces, me, 0, keepdims=False)
    for step in range(1, parts):
        send = lax.dynamic_index_in_dim(pieces, (me + step) % parts, 0, keepdims=False)
        total = total + shifted(send, "op", step)
    return total[None]


def solution(mesh):
    in_specs = (
        P("sec", "op", None, None),
        P("sec", None, None, None),
        P("op", None, None),
        P("op", None),
        P(),
        P(),
    )
    out_specs = P("sec", "op", None, None)
    return jax.shard_map(local, mesh=mesh, in_specs=in_specs, out_specs=out_specs, check_vma=False)
```

```python
import jax
import jax.numpy as jnp
from jax import lax
from jax.experimental import pallas as pl
from jax.experimental.pallas import tpu as pltpu
from jax.sharding import PartitionSpec as P

ROWS = 4
PRECISION = lax.Precision.HIGH


def shifted(value, axis, steps):
    count = lax.axis_size(axis)
    pairs = [(source, (source + steps) % count) for source in range(count)]
    return lax.ppermute(value, axis, pairs)


def sector_steps(sectors):
    return (0, 1, sectors // 2, sectors - 1)


def split_dot(left_parts, right):
    both, left_hi = left_parts
    rows = left_hi.shape[0]
    right_hi = right.astype(jnp.bfloat16)
    right_lo = (right - right_hi.astype(jnp.float32)).astype(jnp.bfloat16)
    first = jnp.dot(both, right_hi, preferred_element_type=jnp.float32)
    second = jnp.dot(left_hi, right_lo, preferred_element_type=jnp.float32)
    return first[:rows] + first[rows:] + second


def transform_kernel(dims_hbm, shift_hbm, env_hbm, mps_hbm, *refs):
    count = len(refs) - 8
    onehot_ref, dims_sc, shift_sc, mps_sc, env_sc, masked_sc, left_sc, half_sc, sems = refs[count - 1:]
    blocks_refs = refs[:count - 1]
    sectors = dims_sc.shape[0]
    states = mps_sc.shape[0]
    channels = env_sc.shape[0]
    width = mps_sc.shape[-1]
    small = [
        pltpu.make_async_copy(dims_hbm, dims_sc, sems.at[0]),
        pltpu.make_async_copy(shift_hbm, shift_sc, sems.at[1]),
        pltpu.make_async_copy(mps_hbm.at[0], mps_sc, sems.at[2]),
    ]
    for copy in small:
        copy.start()
    loads = []
    for j in range(channels):
        copy = pltpu.make_async_copy(env_hbm.at[0, j], env_sc.at[j], sems.at[3 + j])
        copy.start()
        loads.append(copy)
    for copy in small:
        copy.wait()
    here = lax.axis_index("sec")
    dims_in = dims_sc[here]
    rows = lax.broadcasted_iota(jnp.int32, (width, width), 0)
    cols = lax.broadcasted_iota(jnp.int32, (width, width), 1)
    lanes = lax.broadcasted_iota(jnp.int32, (1, states), 1)
    for k, step in enumerate(sector_steps(sectors)):
        pick = 0
        for s in range(states):
            pick = pick + jnp.where(lax.rem(shift_sc[s], sectors) == step, s, 0)
        dims_out = dims_sc[lax.rem(here + step, sectors)]
        live = (rows < dims_in) & (cols < dims_out)
        masked = jnp.where(live, mps_sc[pick], 0.0)
        masked_sc[k] = masked
        left_sc[k * ROWS:(k + 1) * ROWS, :] = jnp.transpose(masked[:, :128])[:ROWS]
        onehot_ref[k:k + 1, :] = (lanes == pick).astype(jnp.float32)
    left = left_sc[...]
    left_hi = left.astype(jnp.bfloat16)
    left_lo = (left - left_hi.astype(jnp.float32)).astype(jnp.bfloat16)
    left_parts = (jnp.concatenate([left_hi, left_lo], axis=0), left_hi)
    for j in range(channels):
        loads[j].wait()
        half = split_dot(left_parts, env_sc[j])
        for k in range(states):
            half_sc[k, j * ROWS:(j + 1) * ROWS, :] = half[k * ROWS:(k + 1) * ROWS]
    for k in range(states):
        full = jnp.dot(half_sc[k], masked_sc[k], precision=PRECISION,
                       preferred_element_type=jnp.float32)
        for j in range(channels):
            blocks_refs[k][j] = full[j * ROWS:(j + 1) * ROWS]


def transform(sector_dims, state_shift, environment, mps):
    channels, width = environment.shape[1], environment.shape[-1]
    states = mps.shape[1]
    anywhere = pl.BlockSpec(memory_space=pl.ANY)
    vmem = pl.BlockSpec(memory_space=pltpu.VMEM)
    flops = 2 * states * ROWS * width * width * channels * 2
    return pl.pallas_call(
        transform_kernel,
        out_shape=tuple(
            jax.ShapeDtypeStruct((channels, ROWS, width), jnp.float32) for _ in range(states)
        ) + (jax.ShapeDtypeStruct((states, states), jnp.float32),),
        in_specs=[anywhere] * 4,
        out_specs=(vmem,) * (states + 1),
        scratch_shapes=[
            pltpu.SMEM(sector_dims.shape, jnp.int32),
            pltpu.SMEM(state_shift.shape, jnp.int32),
            pltpu.VMEM((states, width, width), jnp.float32),
            pltpu.VMEM((channels, width, width), jnp.float32),
            pltpu.VMEM((states, width, width), jnp.float32),
            pltpu.VMEM((states * ROWS, width), jnp.float32),
            pltpu.VMEM((states, channels * ROWS, width), jnp.float32),
            pltpu.SemaphoreType.DMA((3 + channels,)),
        ],
        cost_estimate=pl.CostEstimate(
            flops=6 * flops, transcendentals=0,
            bytes_accessed=4 * (environment.size + mps.size + states * channels * ROWS * width)),
    )(sector_dims, state_shift, environment, mps)


def local(environment, mps, mpo, mpo_pattern, state_shift, sector_dims):
    highest = lax.Precision.HIGHEST
    sectors = lax.axis_size("sec")
    parts = lax.axis_size("op")
    me = lax.axis_index("op")
    *blocks, onehot = transform(sector_dims, state_shift, environment, mps)
    routed = [blocks[0]]
    for k, step in enumerate(sector_steps(sectors)):
        if k:
            routed.append(shifted(blocks[k], "sec", step))
    coef = mpo * mpo_pattern[:, :, None].astype(jnp.float32)
    chosen = jnp.sum(onehot[:, None, :, None] * coef[None], axis=2)
    partial = None
    for k, block in enumerate(routed):
        term = jnp.einsum("wrc,wv->vrc", block, chosen[k], precision=highest)
        partial = term if partial is None else partial + term
    chunk = partial.shape[0] // parts
    pieces = partial.reshape((parts, chunk) + partial.shape[1:])
    total = lax.dynamic_index_in_dim(pieces, me, 0, keepdims=False)
    for step in range(1, parts):
        send = lax.dynamic_index_in_dim(pieces, (me + step) % parts, 0, keepdims=False)
        total = total + shifted(send, "op", step)
    return total[None]


def solution(mesh):
    in_specs = (
        P("sec", "op", None, None),
        P("sec", None, None, None),
        P("op", None, None),
        P("op", None),
        P(),
        P(),
    )
    out_specs = P("sec", "op", None, None)
    return jax.shard_map(local, mesh=mesh, in_specs=in_specs, out_specs=out_specs, check_vma=False)
```

```python
import jax
import jax.numpy as jnp
from jax import lax
from jax.experimental import pallas as pl
from jax.experimental.pallas import tpu as pltpu
from jax.sharding import PartitionSpec as P

ROWS = 4
PRECISION = lax.Precision.HIGH


def shifted(value, axis, steps):
    count = lax.axis_size(axis)
    pairs = [(source, (source + steps) % count) for source in range(count)]
    return lax.ppermute(value, axis, pairs)


def sector_steps(sectors):
    return (0, 1, sectors // 2, sectors - 1)


def split_dot(left_parts, right):
    both, left_hi = left_parts
    rows = left_hi.shape[0]
    right_hi = right.astype(jnp.bfloat16)
    right_lo = (right - right_hi.astype(jnp.float32)).astype(jnp.bfloat16)
    first = jnp.dot(both, right_hi, preferred_element_type=jnp.float32)
    second = jnp.dot(left_hi, right_lo, preferred_element_type=jnp.float32)
    return first[:rows] + first[rows:] + second


def transform_kernel(dims_hbm, shift_hbm, env_hbm, mps_hbm, *refs):
    count = len(refs) - 8
    onehot_ref, dims_sc, shift_sc, mps_sc, env_sc, masked_sc, left_sc, half_sc, sems = refs[count - 1:]
    blocks_refs = refs[:count - 1]
    sectors = dims_sc.shape[0]
    states = mps_sc.shape[0]
    channels = env_sc.shape[0]
    width = mps_sc.shape[-1]
    small = [
        pltpu.make_async_copy(dims_hbm, dims_sc, sems.at[0]),
        pltpu.make_async_copy(shift_hbm, shift_sc, sems.at[1]),
        pltpu.make_async_copy(mps_hbm.at[0], mps_sc, sems.at[2]),
    ]
    for copy in small:
        copy.start()
    loads = []
    for j in range(channels):
        copy = pltpu.make_async_copy(env_hbm.at[0, j], env_sc.at[j], sems.at[3 + j])
        copy.start()
        loads.append(copy)
    for copy in small:
        copy.wait()
    here = lax.axis_index("sec")
    dims_in = dims_sc[here]
    rows = lax.broadcasted_iota(jnp.int32, (width, width), 0)
    cols = lax.broadcasted_iota(jnp.int32, (width, width), 1)
    lanes = lax.broadcasted_iota(jnp.int32, (1, states), 1)
    for k, step in enumerate(sector_steps(sectors)):
        pick = 0
        for s in range(states):
            pick = pick + jnp.where(lax.rem(shift_sc[s], sectors) == step, s, 0)
        dims_out = dims_sc[lax.rem(here + step, sectors)]
        live = (rows < dims_in) & (cols < dims_out)
        masked = jnp.where(live, mps_sc[pick], 0.0)
        masked_sc[k] = masked
        left_sc[k * ROWS:(k + 1) * ROWS, :] = jnp.transpose(masked[:, :128])[:ROWS]
        onehot_ref[k:k + 1, :] = (lanes == pick).astype(jnp.float32)
    left = left_sc[...]
    left_hi = left.astype(jnp.bfloat16)
    left_lo = (left - left_hi.astype(jnp.float32)).astype(jnp.bfloat16)
    left_parts = (jnp.concatenate([left_hi, left_lo], axis=0), left_hi)
    for j in range(channels):
        loads[j].wait()
        half = split_dot(left_parts, env_sc[j])
        for k in range(states):
            half_sc[k, j * ROWS:(j + 1) * ROWS, :] = half[k * ROWS:(k + 1) * ROWS]
    for k in range(states):
        full = jnp.dot(half_sc[k], masked_sc[k], precision=PRECISION,
                       preferred_element_type=jnp.float32)
        for j in range(channels):
            blocks_refs[k][j] = full[j * ROWS:(j + 1) * ROWS]


def transform(sector_dims, state_shift, environment, mps):
    channels, width = environment.shape[1], environment.shape[-1]
    states = mps.shape[1]
    anywhere = pl.BlockSpec(memory_space=pl.ANY)
    vmem = pl.BlockSpec(memory_space=pltpu.VMEM)
    flops = 2 * states * ROWS * width * width * channels * 2
    return pl.pallas_call(
        transform_kernel,
        out_shape=tuple(
            jax.ShapeDtypeStruct((channels, ROWS, width), jnp.float32) for _ in range(states)
        ) + (jax.ShapeDtypeStruct((states, states), jnp.float32),),
        in_specs=[anywhere] * 4,
        out_specs=(vmem,) * (states + 1),
        scratch_shapes=[
            pltpu.SMEM(sector_dims.shape, jnp.int32),
            pltpu.SMEM(state_shift.shape, jnp.int32),
            pltpu.VMEM((states, width, width), jnp.float32),
            pltpu.VMEM((channels, width, width), jnp.float32),
            pltpu.VMEM((states, width, width), jnp.float32),
            pltpu.VMEM((states * ROWS, width), jnp.float32),
            pltpu.VMEM((states, channels * ROWS, width), jnp.float32),
            pltpu.SemaphoreType.DMA((3 + channels,)),
        ],
        cost_estimate=pl.CostEstimate(
            flops=6 * flops, transcendentals=0,
            bytes_accessed=4 * (environment.size + mps.size + states * channels * ROWS * width)),
    )(sector_dims, state_shift, environment, mps)


def local(environment, mps, mpo, mpo_pattern, state_shift, sector_dims):
    highest = lax.Precision.HIGHEST
    sectors = lax.axis_size("sec")
    parts = lax.axis_size("op")
    me = lax.axis_index("op")
    *blocks, onehot = transform(sector_dims, state_shift, environment, mps)
    routed = [blocks[0]]
    for k, step in enumerate(sector_steps(sectors)):
        if k:
            routed.append(shifted(blocks[k], "sec", step))
    coef = mpo * mpo_pattern[:, :, None].astype(jnp.float32)
    chosen = jnp.sum(onehot[:, None, :, None] * coef[None], axis=2)
    partial = None
    for k, block in enumerate(routed):
        term = jnp.einsum("wrc,wv->vrc", block, chosen[k], precision=lax.Precision.HIGH)
        partial = term if partial is None else partial + term
    chunk = partial.shape[0] // parts
    pieces = partial.reshape((parts, chunk) + partial.shape[1:])
    total = lax.dynamic_index_in_dim(pieces, me, 0, keepdims=False)
    for step in range(1, parts):
        send = lax.dynamic_index_in_dim(pieces, (me + step) % parts, 0, keepdims=False)
        total = total + shifted(send, "op", step)
    return total[None]


def solution(mesh):
    in_specs = (
        P("sec", "op", None, None),
        P("sec", None, None, None),
        P("op", None, None),
        P("op", None),
        P(),
        P(),
    )
    out_specs = P("sec", "op", None, None)
    return jax.shard_map(local, mesh=mesh, in_specs=in_specs, out_specs=out_specs, check_vma=False)
```

```python
import jax
import jax.numpy as jnp
from jax import lax
from jax.experimental import pallas as pl
from jax.experimental.pallas import tpu as pltpu
from jax.sharding import PartitionSpec as P

ROWS = 4
PRECISION = lax.Precision.HIGH
GRID = 2


def shifted(value, axis, steps):
    count = lax.axis_size(axis)
    pairs = [(source, (source + steps) % count) for source in range(count)]
    return lax.ppermute(value, axis, pairs)


def sector_steps(sectors):
    return (0, 1, sectors // 2, sectors - 1)


def split_dot(left_parts, right):
    both, left_hi = left_parts
    rows = left_hi.shape[0]
    right_hi = right.astype(jnp.bfloat16)
    right_lo = (right - right_hi.astype(jnp.float32)).astype(jnp.bfloat16)
    first = jnp.dot(both, right_hi, preferred_element_type=jnp.float32)
    second = jnp.dot(left_hi, right_lo, preferred_element_type=jnp.float32)
    return first[:rows] + first[rows:] + second


def transform_kernel(dims_hbm, shift_hbm, env_ref, mps_ref, *refs):
    count = len(refs) - 7
    blocks_refs = refs[:count]
    onehot_ref, dims_sc, shift_sc, masked_sc, left_sc, half_sc, sems = refs[count:]
    sectors = dims_sc.shape[0]
    states = mps_ref.shape[1]
    block_channels = env_ref.shape[1]
    steps_total = pl.num_programs(0)
    width = mps_ref.shape[-1]
    here = lax.axis_index("sec")
    step = pl.program_id(0)

    @pl.when(step == 0)
    def _():
        small = [
            pltpu.make_async_copy(dims_hbm, dims_sc, sems.at[0]),
            pltpu.make_async_copy(shift_hbm, shift_sc, sems.at[1]),
        ]
        for copy in small:
            copy.start()
        for copy in small:
            copy.wait()
        dims_in = dims_sc[here]
        rows = lax.broadcasted_iota(jnp.int32, (width, width), 0)
        cols = lax.broadcasted_iota(jnp.int32, (width, width), 1)
        lanes = lax.broadcasted_iota(jnp.int32, (1, states), 1)
        for k, shift in enumerate(sector_steps(sectors)):
            pick = 0
            for s in range(states):
                pick = pick + jnp.where(lax.rem(shift_sc[s], sectors) == shift, s, 0)
            dims_out = dims_sc[lax.rem(here + shift, sectors)]
            live = (rows < dims_in) & (cols < dims_out)
            masked = jnp.where(live, mps_ref[0, pick], 0.0)
            masked_sc[k] = masked
            left_sc[k * ROWS:(k + 1) * ROWS, :] = jnp.transpose(masked[:, :128])[:ROWS]
            onehot_ref[k:k + 1, :] = (lanes == pick).astype(jnp.float32)

    left = left_sc[...]
    left_hi = left.astype(jnp.bfloat16)
    left_lo = (left - left_hi.astype(jnp.float32)).astype(jnp.bfloat16)
    left_parts = (jnp.concatenate([left_hi, left_lo], axis=0), left_hi)
    for block_index in range(half_sc.shape[1] // ROWS // block_channels):
        @pl.when(step == block_index)
        def _():
            for jj in range(block_channels):
                j = block_index * block_channels + jj
                half = split_dot(left_parts, env_ref[0, jj])
                for k in range(states):
                    half_sc[k, j * ROWS:(j + 1) * ROWS, :] = half[k * ROWS:(k + 1) * ROWS]

    @pl.when(step == steps_total - 1)
    def _():
        channels = half_sc.shape[1] // ROWS
        for k in range(states):
            full = jnp.dot(half_sc[k], masked_sc[k], precision=PRECISION,
                           preferred_element_type=jnp.float32)
            for j in range(channels):
                blocks_refs[k][j] = full[j * ROWS:(j + 1) * ROWS]


def transform(sector_dims, state_shift, environment, mps):
    channels, width = environment.shape[1], environment.shape[-1]
    states = mps.shape[1]
    grid = GRID if channels % GRID == 0 else 1
    block_channels = channels // grid
    anywhere = pl.BlockSpec(memory_space=pl.ANY)
    whole = lambda shape: pl.BlockSpec(shape, lambda i: (0,) * len(shape))
    flops = 2 * states * ROWS * width * width * channels * 2
    return pl.pallas_call(
        transform_kernel,
        grid=(grid,),
        out_shape=tuple(
            jax.ShapeDtypeStruct((channels, ROWS, width), jnp.float32) for _ in range(states)
        ) + (jax.ShapeDtypeStruct((states, states), jnp.float32),),
        in_specs=[
            anywhere, anywhere,
            pl.BlockSpec((1, block_channels, width, width), lambda i: (0, i, 0, 0)),
            whole((1, states, width, width)),
        ],
        out_specs=tuple(whole((channels, ROWS, width)) for _ in range(states))
        + (whole((states, states)),),
        scratch_shapes=[
            pltpu.SMEM(sector_dims.shape, jnp.int32),
            pltpu.SMEM(state_shift.shape, jnp.int32),
            pltpu.VMEM((states, width, width), jnp.float32),
            pltpu.VMEM((states * ROWS, width), jnp.float32),
            pltpu.VMEM((states, channels * ROWS, width), jnp.float32),
            pltpu.SemaphoreType.DMA((2,)),
        ],
        cost_estimate=pl.CostEstimate(
            flops=6 * flops, transcendentals=0,
            bytes_accessed=4 * (environment.size + mps.size + states * channels * ROWS * width)),
    )(sector_dims, state_shift, environment, mps)


def local(environment, mps, mpo, mpo_pattern, state_shift, sector_dims):
    highest = lax.Precision.HIGHEST
    sectors = lax.axis_size("sec")
    parts = lax.axis_size("op")
    me = lax.axis_index("op")
    *blocks, onehot = transform(sector_dims, state_shift, environment, mps)
    routed = [blocks[0]]
    for k, step in enumerate(sector_steps(sectors)):
        if k:
            routed.append(shifted(blocks[k], "sec", step))
    coef = mpo * mpo_pattern[:, :, None].astype(jnp.float32)
    chosen = jnp.sum(onehot[:, None, :, None] * coef[None], axis=2)
    partial = None
    for k, block in enumerate(routed):
        term = jnp.einsum("wrc,wv->vrc", block, chosen[k], precision=lax.Precision.HIGH)
        partial = term if partial is None else partial + term
    chunk = partial.shape[0] // parts
    pieces = partial.reshape((parts, chunk) + partial.shape[1:])
    total = lax.dynamic_index_in_dim(pieces, me, 0, keepdims=False)
    for step in range(1, parts):
        send = lax.dynamic_index_in_dim(pieces, (me + step) % parts, 0, keepdims=False)
        total = total + shifted(send, "op", step)
    return total[None]


def solution(mesh):
    in_specs = (
        P("sec", "op", None, None),
        P("sec", None, None, None),
        P("op", None, None),
        P("op", None),
        P(),
        P(),
    )
    out_specs = P("sec", "op", None, None)
    return jax.shard_map(local, mesh=mesh, in_specs=in_specs, out_specs=out_specs, check_vma=False)
```
